32 devices in a mesh: section: 4 (over z), tensor: 8 (over y, x, core).
Axes of the slice: x: 2, y: 2, z: 4, core: 2. Of those that a mesh axis runs over, the one named last changes fastest.
Arguments:
- resid: bfloat16 [32, 3584], P('tensor'), may hold values from -6 to 6
- w_enc: bfloat16 [7168, 3584], P(('section', 'tensor')), may hold values from -0.09375 to 0.09375
- b_enc: float32 [7168], P(('section', 'tensor')), may hold values from -1 to 0.5
- w_dec: bfloat16 [7168, 3584], P(('section', 'tensor')), may hold values from -0.0625 to 0.0625
- b_dec: float32 [3584], replicated, may hold values from -3 to 3
Outputs:
- recon: float32 [32, 3584], P('tensor')
- grad_w_dec: bfloat16 [7168, 3584], P(('section', 'tensor'))
- code_grad: float32 [32, 7168], P(None, ('section', 'tensor'))
- grad_b_dec: float32 [3584], replicated
- loss_value: float32 [], replicated
The draws below stay inside these ranges and needn't reach their ends.
All inputs are finite; a program needn't handle non-finite values.
Results may differ from the reference program's by a relative error of at most 0.0032.
The reference program's roundings to bfloat16 on the way (of `codes` and `err_half`) count: a program that leaves them out, or rounds other values in their place, can miss the bound.
Values may be sent and summed in bfloat16 or wider, within the bound.
No kernel may reach another device: no remote copies, remote signals or barrier semaphores. Data moves between devices by JAX's collectives and lax.ppermute only.
A program may use at most 64 MiB of HBM per device.

```python
import jax
import jax.numpy as jnp
from jax import lax

D = 3584
LAT_DEV = 224
ROWS = 32
LATENTS = 7168
N_SECTION = 4
N_TENSOR = 8


def block_levels(rng, extent, split, low, high):
    loudness, own = 1.0, jax.random.fold_in(rng, 6)
    for dim, blocks in split:
        steps = jnp.exp(jax.random.uniform(jax.random.fold_in(own, dim), (blocks,), jnp.float32, low / len(split), high / len(split)))
        loudness = loudness * jnp.repeat(steps, extent[dim] // blocks).reshape([-1 if axis == dim else 1 for axis in range(len(extent))])
    return loudness


def bell_draw(rng, dims, width, limit, shards=(), held_as=jnp.bfloat16):
    gain = block_levels(rng, dims, shards, -0.22, 0.18) if shards else 1.0
    result = jax.random.normal(rng, dims, jnp.float32) * width * gain
    return jnp.minimum(jnp.maximum(result, -limit), limit).astype(held_as)


def setup_inputs(seed: int = 0) -> dict:
    seeds = jax.random.split(jax.random.key(seed), 6)
    resid = bell_draw(seeds[0], (ROWS, D), 1.0, 6.0, ((0, 8),))
    w_enc = bell_draw(seeds[1], (LATENTS, D), D ** -0.5, 0.09375, ((0, 32),))
    b_enc = jnp.clip(-1.0 + 1.5 * jax.random.uniform(seeds[2], (LATENTS,), jnp.float32) ** block_levels(seeds[2], (LATENTS,), ((0, 32),), -0.2, 0.2), -1.0, 0.5)
    w_dec = bell_draw(seeds[3], (LATENTS, D), LATENTS ** -0.5, 0.0625, ((0, 32),))
    b_dec = bell_draw(seeds[4], (D,), 0.5, 3.0, (), jnp.float32)
    return dict(resid=resid, w_enc=w_enc, b_enc=b_enc, w_dec=w_dec, b_dec=b_dec)


epsilon = 1e-06

def block_codes(resid, enc_block, bias_block):
    preact = lax.dot_general(resid, enc_block, (((1,), (1,)), ((), ())), preferred_element_type=jnp.float32) + bias_block
    return jnp.maximum(preact, 0.0).astype(jnp.bfloat16)

def block_norm(dec_block):
    dec_f32 = dec_block.astype(jnp.float32)
    return (dec_f32, jnp.sqrt(lax.optimization_barrier(jnp.sum(dec_f32 * dec_f32, axis=1)) + epsilon))

def reference(resid, w_enc, b_enc, w_dec, b_dec):
    blocks = N_SECTION * N_TENSOR
    enc_blocks = w_enc.reshape(blocks, LAT_DEV, D)
    bias_blocks = b_enc.reshape(blocks, LAT_DEV)
    dec_blocks = w_dec.reshape(blocks, LAT_DEV, D)

    def forward(carry, pieces):
        enc_block, bias_block, dec_block = pieces
        codes = block_codes(resid, enc_block, bias_block)
        dec_f32, dec_norm = block_norm(dec_block)
        total, penalty = carry
        total = total + jnp.dot(codes, dec_block, preferred_element_type=jnp.float32)
        penalty = penalty + jnp.sum(codes.astype(jnp.float32) * dec_norm)
        return ((total, penalty), None)
    start = (jnp.zeros((ROWS, D), jnp.float32), jnp.zeros((), jnp.float32))
    (summed, penalty), unused = lax.scan(forward, start, (enc_blocks, bias_blocks, dec_blocks))
    recon = summed + b_dec
    errors = recon - resid.astype(jnp.float32)
    loss_value = (0.5 * jnp.sum(errors * errors) + penalty) / (ROWS * D)
    err_half = errors.astype(jnp.bfloat16)

    def backward(pieces):
        enc_block, bias_block, dec_block = pieces
        codes = block_codes(resid, enc_block, bias_block)
        dec_f32, dec_norm = block_norm(dec_block)
        code_sums = lax.optimization_barrier(jnp.sum(codes.astype(jnp.float32), axis=0))
        grad_block = lax.dot_general(codes, err_half, (((0,), (0,)), ((), ())), preferred_element_type=jnp.float32)
        grad_block = grad_block + code_sums[:, None] * dec_f32 / dec_norm[:, None]
        code_block = lax.dot_general(err_half, dec_block, (((1,), (1,)), ((), ())), preferred_element_type=jnp.float32) + dec_norm
        return (grad_block.astype(jnp.bfloat16), code_block)
    grad_blocks, code_blocks = lax.map(backward, (enc_blocks, bias_blocks, dec_blocks))
    grad_w_dec = grad_blocks.reshape(LATENTS, D)
    code_grad = jnp.transpose(code_blocks, (1, 0, 2)).reshape(ROWS, LATENTS)
    grad_b_dec = lax.optimization_barrier(jnp.sum(errors, axis=0))
    return (recon, grad_w_dec, code_grad, grad_b_dec, loss_value)
```

```python
import jax
import jax.numpy as jnp
from jax import lax
from jax.sharding import PartitionSpec as P

epsilon = 1e-06


def swap(x, axis, size, mask):
    return lax.ppermute(x, axis, [(i, i ^ mask) for i in range(size)])


def far_masks(size):
    return [0] + list(range(3, size, 2))


def tree_sum(terms):
    while len(terms) > 1:
        terms = [terms[i] + terms[i + 1] for i in range(0, len(terms), 2)]
    return terms[0]


def gather_relative(x, axis, size):
    far = jnp.stack([x] + [swap(x, axis, size, m) for m in far_masks(size)[1:]])
    return jnp.concatenate([far, swap(far, axis, size, 1)])


def pieces(x):
    high = lax.reduce_precision(x, 8, 7)
    rest = x - high
    middle = lax.reduce_precision(rest, 8, 7)
    return [p.astype(jnp.bfloat16) for p in (high, middle, rest - middle)]


def per_device(n_section, n_tensor, resid, w_enc, b_enc, w_dec, b_dec):
    rows, width = resid.shape
    lat = w_enc.shape[0]
    masks = far_masks(n_tensor)
    order = masks + [m ^ 1 for m in masks]
    half = len(masks)

    dec_f32 = w_dec.astype(jnp.float32)
    dec_norm = jnp.sqrt(jnp.sum(dec_f32 * dec_f32, axis=1) + epsilon)
    stream = gather_relative(resid, "tensor", n_tensor).reshape(-1, width)
    total_rows = stream.shape[0]
    preact = (
        lax.dot_general(stream, w_enc, (((1,), (1,)), ((), ())), preferred_element_type=jnp.float32)
        + b_enc
    )
    codes = jnp.maximum(preact, 0.0).astype(jnp.bfloat16)
    codes_f32 = codes.astype(jnp.float32)
    penalty = jnp.sum(codes_f32 * dec_norm)
    partial = jnp.dot(codes, w_dec, preferred_element_type=jnp.float32)
    partial = partial.reshape(2, half, rows, width)
    pair = partial[0] + swap(partial[1], "tensor", n_tensor, 1)
    share = pair[0]
    for k, m in enumerate(masks[1:], 1):
        share = share + swap(pair[k], "tensor", n_tensor, m)
    share = jnp.concatenate([share, jnp.full((rows, 128), penalty)], axis=1)
    share = tree_sum([share] + [swap(share, "section", n_section, m) for m in range(1, n_section)])
    recon = share[:, :width] + b_dec
    penalty = share[0, width]
    errors = recon - resid.astype(jnp.float32)
    squares = jnp.sum(errors * errors)
    column = jnp.sum(errors, axis=0)
    scalars = jnp.zeros((width,), jnp.bfloat16)
    for k, p in enumerate(pieces(0.5 * squares + penalty)):
        scalars = scalars.at[128 * k].set(p)
    payload = jnp.concatenate(
        [errors.astype(jnp.bfloat16), jnp.stack(pieces(column)[:2] + [scalars])], axis=0
    )
    blocks = gather_relative(payload, "tensor", n_tensor)
    err_half = blocks[:, :rows].reshape(total_rows, width)
    by_mask = [blocks[order.index(m), rows:].astype(jnp.float32) for m in range(n_tensor)]
    grad_b_dec = tree_sum([b[0] + b[1] for b in by_mask])
    loss_value = tree_sum([b[2, 0] + b[2, 128] + b[2, 256] for b in by_mask])
    loss_value = loss_value / (total_rows * width)
    code_sums = jnp.sum(codes_f32, axis=0)
    grad_w_dec = lax.dot_general(
        codes, err_half, (((0,), (0,)), ((), ())), preferred_element_type=jnp.float32
    )
    grad_w_dec = grad_w_dec + code_sums[:, None] * dec_f32 / dec_norm[:, None]
    code_grad = (
        lax.dot_general(
            err_half, w_dec, (((1,), (1,)), ((), ())), preferred_element_type=jnp.float32
        )
        + dec_norm
    )
    me = lax.axis_index("tensor")
    code_grad = code_grad.reshape(n_tensor, rows, lat)
    place = jnp.array([order.index(m) for m in range(n_tensor)])[me ^ jnp.arange(n_tensor)]
    code_grad = code_grad[place].reshape(total_rows, lat)
    return (recon, grad_w_dec.astype(jnp.bfloat16), code_grad, grad_b_dec, loss_value)


def solution(mesh):
    n_section, n_tensor = mesh.shape["section"], mesh.shape["tensor"]
    in_specs = (
        P("tensor", None),
        P(("section", "tensor"), None),
        P(("section", "tensor")),
        P(("section", "tensor"), None),
        P(),
    )
    out_specs = (
        P("tensor", None),
        P(("section", "tensor"), None),
        P(None, ("section", "tensor")),
        P(),
        P(),
    )

    def body(*args):
        return per_device(n_section, n_tensor, *args)

    return jax.shard_map(body, mesh=mesh, in_specs=in_specs, out_specs=out_specs, check_vma=False)
```

```python
import functools

import jax
import jax.numpy as jnp
from jax import lax
from jax.experimental import pallas as pl
from jax.experimental.pallas import tpu as pltpu
from jax.sharding import PartitionSpec as P

epsilon = 1e-06
LANES = 128


BF16, F32 = jnp.bfloat16, jnp.float32
VMEM = pl.BlockSpec(memory_space=pltpu.VMEM)
PARAMS = pltpu.CompilerParams(vmem_limit_bytes=16 << 20)


def swap(x, axis, size, mask):
    return lax.ppermute(x, axis, [(i, i ^ mask) for i in range(size)])


def far_masks(size):
    return [0] + list(range(3, size, 2))


def tree_sum(terms):
    while len(terms) > 1:
        terms = [terms[i] + terms[i + 1] for i in range(0, len(terms), 2)]
    return terms[0]


def chunk_of(width):
    return next(c for c in (512, 384, 256, 128) if width % c == 0)


def contract(a, b, dims):
    return lax.dot_general(a, b, (dims, ((), ())), preferred_element_type=F32)


def prepare_kernel(dec_ref, bias_ref, resid_ref, norm_ref, bias_col_ref, own_ref):
    lat, width = dec_ref.shape
    total = jnp.zeros((lat, LANES), F32)
    for c in range(0, width, LANES):
        part = dec_ref[:, c : c + LANES].astype(F32)
        total = total + part * part
    norm_ref[...] = jnp.sqrt(jnp.sum(total, axis=1, keepdims=True) + epsilon)
    bias_col_ref[...] = jnp.transpose(jnp.broadcast_to(bias_ref[...], (8, lat)))[:, :1]
    own_ref[...] = resid_ref[...]


def forward_kernel(
    near_ref, other_ref, enc_ref, bias_ref, dec_ref, norm_ref,
    keep_ref, send_ref, codes_ref, scale_ref, rows_f32,
):
    half, rows, width = near_ref.shape
    for p in range(2 * half):
        block = near_ref[p] if p < half else other_ref[p - half]
        rows_f32[p * rows : (p + 1) * rows, :] = block.astype(F32)
    stream = rows_f32[...].astype(BF16)
    preact = contract(enc_ref[...], stream, ((1,), (1,))) + bias_ref[...]
    codes = jnp.maximum(preact, 0.0).astype(BF16)
    codes_ref[...] = codes
    codes_f32 = codes.astype(F32)
    norm = norm_ref[...]
    scale_ref[...] = jnp.sum(codes_f32, axis=1, keepdims=True) / norm
    penalty = jnp.sum(codes_f32 * norm, axis=(0, 1), keepdims=True)
    tail = jnp.broadcast_to(penalty, (rows, LANES))
    by_row = jnp.transpose(codes_f32).astype(BF16)
    for out_ref in (keep_ref, send_ref):
        for k in range(half):
            out_ref[k, :, width:] = tail
    chunk = chunk_of(width)
    for c in range(0, width, chunk):
        part = contract(by_row, dec_ref[:, c : c + chunk], ((1,), (0,)))
        for p in range(2 * half):
            out_ref = keep_ref if p < half else send_ref
            out_ref[p % half, :, c : c + chunk] = part[p * rows : (p + 1) * rows]


def error_kernel(n_tensor, n_terms, *refs):
    terms, (bias_ref, resid_ref, recon_ref, out_ref, pack) = refs[:n_terms], refs[n_terms:]
    rows, width = resid_ref.shape
    cut, piece = width // 2, width // rows
    total = tree_sum([t[...] for t in terms])
    recon = total[:, :width] + bias_ref[...]
    recon_ref[...] = recon
    errors = recon - resid_ref[...].astype(F32)
    column = jnp.sum(errors, axis=0, keepdims=True)
    squares = jnp.sum(errors * errors, axis=(0, 1), keepdims=True)
    value = 0.5 * squares + total[:1, width : width + 1] * (1.0 / n_tensor)
    pack[:rows, :cut] = errors[:, :cut]
    pack[rows:, :cut] = errors[:, cut:]
    high = column.astype(BF16).astype(F32)
    low = column - high
    for r in range(rows):
        pack[r : r + 1, cut : cut + piece] = high[:, r * piece : (r + 1) * piece]
        pack[rows + r : rows + r + 1, cut : cut + piece] = low[:, r * piece : (r + 1) * piece]
    pack[:, cut + piece :] = jnp.zeros((2 * rows, LANES), F32)
    for r in range(3):
        high = value.astype(BF16).astype(F32)
        pack[r : r + 1, cut + piece :] = jnp.broadcast_to(high, (1, LANES))
        value = value - high
    out_ref[...] = pack[...].astype(BF16)


def backward_kernel(
    order, near_ref, other_ref, codes_ref, scale_ref, dec_ref, norm_ref,
    grad_ref, code_grad_ref, column_ref, loss_ref, rows_f32, staged, sems,
):
    half, rows2, packed = near_ref.shape
    rows = rows2 // 2
    lat, width = dec_ref.shape
    cut, piece = width // 2, width // rows
    columns, losses = {}, {}
    for p, mask in enumerate(order):
        block = (near_ref[p] if p < half else other_ref[p - half]).astype(F32)
        rows_f32[p * rows : (p + 1) * rows, :cut] = block[:rows, :cut]
        rows_f32[p * rows : (p + 1) * rows, cut:] = block[rows:, :cut]
        columns[mask] = block[:rows, cut : cut + piece] + block[rows:, cut : cut + piece]
        ends = block[:, cut + piece : cut + piece + 1]
        losses[mask] = (ends[0:1] + ends[1:2]) + ends[2:3]
    errors = rows_f32[...].astype(BF16)
    codes, scale = codes_ref[...], scale_ref[...]
    chunk = staged.shape[2]
    copies = []
    for i in range(width // chunk):
        cols = slice(i * chunk, (i + 1) * chunk)
        grad = contract(codes, errors[:, cols], ((1,), (0,)))
        staged[i] = (grad + scale * dec_ref[:, cols].astype(F32)).astype(BF16)
        copies.append(pltpu.make_async_copy(staged.at[i], grad_ref.at[:, cols], sems.at[i]))
        copies[-1].start()
    by_lat = contract(dec_ref[...], errors, ((1,), (1,))) + norm_ref[...]
    by_row = jnp.transpose(by_lat)
    me = lax.axis_index("tensor")
    for p, mask in enumerate(order[:half]):
        block = lax.bitwise_xor(me, mask)
        one = by_row[p * rows : (p + 1) * rows]
        two = by_row[(half + p) * rows : (half + p + 1) * rows]
        if len(code_grad_ref.shape) == 3:
            code_grad_ref[block] = one
            code_grad_ref[lax.bitwise_xor(block, 1)] = two
        else:
            odd = lax.rem(block, 2) == 1
            both = jnp.concatenate([jnp.where(odd, two, one), jnp.where(odd, one, two)])
            start = pl.multiple_of(lax.div(block, 2) * 2 * rows, 2 * rows)
            code_grad_ref[pl.ds(start, 2 * rows), :] = both
    column = tree_sum([columns[m] for m in range(len(order))])
    for r in range(rows):
        column_ref[r * piece : (r + 1) * piece] = column[r]
    loss_ref[...] = tree_sum([losses[m] for m in range(len(order))]) / (len(order) * rows * width)
    for copy in copies:
        copy.wait()


def per_device(n_section, n_tensor, resid, w_enc, b_enc, w_dec, b_dec):
    rows, width = resid.shape
    lat = w_enc.shape[0]
    masks = far_masks(n_tensor)
    order = masks + [m ^ 1 for m in masks]
    half = len(masks)
    total_rows = n_tensor * rows
    wide = width + LANES
    shape = jax.ShapeDtypeStruct

    norm, bias, own = pl.pallas_call(
        prepare_kernel,
        out_shape=(shape((lat, 1), F32), shape((lat, 1), F32), shape((rows, width), BF16)),
        in_specs=[VMEM] * 3,
        out_specs=(VMEM,) * 3,
        compiler_params=PARAMS,
    )(w_dec, b_enc.reshape(1, lat), resid)
    near = jnp.stack([own] + [swap(resid, "tensor", n_tensor, m) for m in masks[1:]])
    near, norm, bias = lax.optimization_barrier((near, norm, bias))
    other = swap(near, "tensor", n_tensor, 1)
    keep, send, codes, scale = pl.pallas_call(
        forward_kernel,
        out_shape=(
            shape((half, rows, wide), F32),
            shape((half, rows, wide), F32),
            shape((lat, total_rows), BF16),
            shape((lat, 1), F32),
        ),
        in_specs=[VMEM] * 6,
        out_specs=(VMEM,) * 4,
        compiler_params=PARAMS,
        scratch_shapes=[pltpu.VMEM((total_rows, width), F32)],
    )(near, other, w_enc, bias, w_dec, norm)
    pair = keep + swap(send, "tensor", n_tensor, 1)
    share = pair[0]
    for k, m in enumerate(masks[1:], 1):
        share = share + swap(pair[k], "tensor", n_tensor, m)
    terms = [share] + [swap(share, "section", n_section, m) for m in range(1, n_section)]
    packed = width // 2 + width // rows + LANES
    recon, payload = pl.pallas_call(
        functools.partial(error_kernel, n_tensor, len(terms)),
        out_shape=(shape((rows, width), F32), shape((2 * rows, packed), BF16)),
        in_specs=[VMEM] * (len(terms) + 2),
        out_specs=(VMEM, VMEM),
        compiler_params=PARAMS,
        scratch_shapes=[pltpu.VMEM((2 * rows, packed), F32)],
    )(*terms, b_dec.reshape(1, width), own)
    near = jnp.stack([payload] + [swap(payload, "tensor", n_tensor, m) for m in masks[1:]])
    other = swap(near, "tensor", n_tensor, 1)
    chunk = chunk_of(width)
    grad_w_dec, code_grad, column, loss = pl.pallas_call(
        functools.partial(backward_kernel, order),
        out_shape=(
            shape((lat, width), BF16),
            shape((total_rows, lat) if rows % 4 == 0 else (n_tensor, rows, lat), F32),
            shape((width,), F32),
            shape((1, 1), F32),
        ),
        in_specs=[VMEM] * 6,
        out_specs=(pl.BlockSpec(memory_space=pl.ANY), VMEM, VMEM, VMEM),
        compiler_params=PARAMS,
        scratch_shapes=[
            pltpu.VMEM((total_rows, width), F32),
            pltpu.VMEM((width // chunk, lat, chunk), BF16),
            pltpu.SemaphoreType.DMA((width // chunk,)),
        ],
    )(near, other, codes, scale, w_dec, norm)
    return recon, grad_w_dec, code_grad.reshape(total_rows, lat), column, loss.reshape(())


def solution(mesh):
    n_section, n_tensor = mesh.shape["section"], mesh.shape["tensor"]
    in_specs = (
        P("tensor", None),
        P(("section", "tensor"), None),
        P(("section", "tensor")),
        P(("section", "tensor"), None),
        P(),
    )
    out_specs = (
        P("tensor", None),
        P(("section", "tensor"), None),
        P(None, ("section", "tensor")),
        P(),
        P(),
    )

    def body(*args):
        return per_device(n_section, n_tensor, *args)

    return jax.shard_map(body, mesh=mesh, in_specs=in_specs, out_specs=out_specs, check_vma=False)
```

```python
import functools

import jax
import jax.numpy as jnp
from jax import lax
from jax.experimental import pallas as pl
from jax.experimental.pallas import tpu as pltpu
from jax.sharding import PartitionSpec as P


epsilon = 1e-06
LANES = 128


BF16, F32 = jnp.bfloat16, jnp.float32
VMEM = pl.BlockSpec(memory_space=pltpu.VMEM)
PARAMS = pltpu.CompilerParams(vmem_limit_bytes=16 << 20)


def swap(x, axis, size, mask):
    return lax.ppermute(x, axis, [(i, i ^ mask) for i in range(size)])


def swaps(xs, axis, size, masks):
    out = []
    for x, m in zip(xs, masks):
        out.append(swap(x, axis, size, m))
    return out


def far_masks(size):
    return [0] + list(range(3, size, 2))


def tree_sum(terms):
    while len(terms) > 1:
        terms = [terms[i] + terms[i + 1] for i in range(0, len(terms), 2)]
    return terms[0]


def chunk_of(width):
    return next(c for c in (512, 384, 256, 128) if width % c == 0)


def contract(a, b, dims):
    return lax.dot_general(a, b, (dims, ((), ())), preferred_element_type=F32)


def prepare_kernel(dec_ref, bias_ref, resid_ref, norm_ref, bias_col_ref, own_ref):
    lat, width = dec_ref.shape
    total = jnp.zeros((lat, LANES), F32)
    for c in range(0, width, LANES):
        part = dec_ref[:, c : c + LANES].astype(F32)
        total = total + part * part
    norm_ref[...] = jnp.sqrt(jnp.sum(total, axis=1, keepdims=True) + epsilon)
    bias_col_ref[...] = jnp.transpose(jnp.broadcast_to(bias_ref[...], (8, lat)))[:, :1]
    own_ref[...] = resid_ref[...]


def forward_kernel(
    near_ref, other_ref, enc_ref, bias_ref, dec_ref, norm_ref,
    keep_ref, send_ref, codes_ref, scale_ref, rows_f32,
):
    half, rows, width = near_ref.shape
    for p in range(2 * half):
        block = near_ref[p] if p < half else other_ref[p - half]
        rows_f32[p * rows : (p + 1) * rows, :] = block.astype(F32)
    stream = rows_f32[...].astype(BF16)
    preact = contract(enc_ref[...], stream, ((1,), (1,))) + bias_ref[...]
    codes = jnp.maximum(preact, 0.0).astype(BF16)
    codes_ref[...] = codes
    codes_f32 = codes.astype(F32)
    norm = norm_ref[...]
    scale_ref[...] = jnp.sum(codes_f32, axis=1, keepdims=True) / norm
    penalty = jnp.sum(codes_f32 * norm, axis=(0, 1), keepdims=True)
    tail = jnp.broadcast_to(penalty, (rows, LANES))
    by_row = jnp.transpose(codes_f32).astype(BF16)
    for out_ref in (keep_ref, send_ref):
        for k in range(half):
            out_ref[k, :, width:] = tail
    chunk = chunk_of(width)
    for c in range(0, width, chunk):
        part = contract(by_row, dec_ref[:, c : c + chunk], ((1,), (0,)))
        for p in range(2 * half):
            out_ref = keep_ref if p < half else send_ref
            out_ref[p % half, :, c : c + chunk] = part[p * rows : (p + 1) * rows]


def error_kernel(n_tensor, n_terms, *refs):
    terms, (bias_ref, resid_ref, recon_ref, out_ref, pack) = refs[:n_terms], refs[n_terms:]
    rows, width = resid_ref.shape
    cut, piece = width // 2, width // rows
    total = tree_sum([t[...] for t in terms])
    recon = total[:, :width] + bias_ref[...]
    recon_ref[...] = recon
    errors = recon - resid_ref[...].astype(F32)
    column = jnp.sum(errors, axis=0, keepdims=True)
    squares = jnp.sum(errors * errors, axis=(0, 1), keepdims=True)
    value = 0.5 * squares + total[:1, width : width + 1] * (1.0 / n_tensor)
    pack[:rows, :cut] = errors[:, :cut]
    pack[rows:, :cut] = errors[:, cut:]
    high = column.astype(BF16).astype(F32)
    low = column - high
    for r in range(rows):
        pack[r : r + 1, cut : cut + piece] = high[:, r * piece : (r + 1) * piece]
        pack[rows + r : rows + r + 1, cut : cut + piece] = low[:, r * piece : (r + 1) * piece]
    pack[:, cut + piece :] = jnp.zeros((2 * rows, LANES), F32)
    for r in range(3):
        high = value.astype(BF16).astype(F32)
        pack[r : r + 1, cut + piece :] = jnp.broadcast_to(high, (1, LANES))
        value = value - high
    out_ref[...] = pack[...].astype(BF16)


def backward_kernel(
    order, near_ref, other_ref, codes_ref, scale_ref, dec_ref, norm_ref,
    grad_ref, code_grad_ref, column_ref, loss_ref, rows_f32, staged, sems,
):
    half, rows2, _ = near_ref.shape
    rows = rows2 // 2
    _, width = dec_ref.shape
    cut, piece = width // 2, width // rows
    columns, losses = {}, {}
    for p, mask in enumerate(order):
        block = (near_ref[p] if p < half else other_ref[p - half]).astype(F32)
        rows_f32[p * rows : (p + 1) * rows, :cut] = block[:rows, :cut]
        rows_f32[p * rows : (p + 1) * rows, cut:] = block[rows:, :cut]
        columns[mask] = block[:rows, cut : cut + piece] + block[rows:, cut : cut + piece]
        ends = block[:, cut + piece : cut + piece + 1]
        losses[mask] = (ends[0:1] + ends[1:2]) + ends[2:3]
    errors = rows_f32[...].astype(BF16)
    codes, scale = codes_ref[...], scale_ref[...]
    chunk = staged.shape[2]
    copies = []
    for i in range(width // chunk):
        cols = slice(i * chunk, (i + 1) * chunk)
        grad = contract(codes, errors[:, cols], ((1,), (0,)))
        staged[i] = (grad + scale * dec_ref[:, cols].astype(F32)).astype(BF16)
        copies.append(pltpu.make_async_copy(staged.at[i], grad_ref.at[:, cols], sems.at[i]))
        copies[-1].start()
    by_lat = contract(dec_ref[...], errors, ((1,), (1,))) + norm_ref[...]
    by_row = jnp.transpose(by_lat)
    me = lax.axis_index("tensor")
    for p, mask in enumerate(order[:half]):
        block = lax.bitwise_xor(me, mask)
        one = by_row[p * rows : (p + 1) * rows]
        two = by_row[(half + p) * rows : (half + p + 1) * rows]
        if len(code_grad_ref.shape) == 3:
            code_grad_ref[block] = one
            code_grad_ref[lax.bitwise_xor(block, 1)] = two
        else:
            odd = lax.rem(block, 2) == 1
            both = jnp.concatenate([jnp.where(odd, two, one), jnp.where(odd, one, two)])
            start = pl.multiple_of(lax.div(block, 2) * 2 * rows, 2 * rows)
            code_grad_ref[pl.ds(start, 2 * rows), :] = both
    column = tree_sum([columns[m] for m in range(len(order))])
    for r in range(rows):
        column_ref[r * piece : (r + 1) * piece] = column[r]
    loss_ref[...] = tree_sum([losses[m] for m in range(len(order))]) / (len(order) * rows * width)
    for copy in copies:
        copy.wait()


def per_device(n_section, n_tensor, resid, w_enc, b_enc, w_dec, b_dec):
    rows, width = resid.shape
    lat = w_enc.shape[0]
    masks = far_masks(n_tensor)
    order = masks + [m ^ 1 for m in masks]
    half = len(masks)
    total_rows = n_tensor * rows
    wide = width + LANES
    shape = jax.ShapeDtypeStruct

    norm, bias, own = pl.pallas_call(
        prepare_kernel,
        out_shape=(shape((lat, 1), F32), shape((lat, 1), F32), shape((rows, width), BF16)),
        in_specs=[VMEM] * 3,
        out_specs=(VMEM,) * 3,
        compiler_params=PARAMS,
    )(w_dec, b_enc.reshape(1, lat), resid)
    near = jnp.stack([own] + swaps([resid] * half, "tensor", n_tensor, masks[1:]))
    near, norm, bias = lax.optimization_barrier((near, norm, bias))
    other = swap(near, "tensor", n_tensor, 1)
    keep, send, codes, scale = pl.pallas_call(
        forward_kernel,
        out_shape=(
            shape((half, rows, wide), F32),
            shape((half, rows, wide), F32),
            shape((lat, total_rows), BF16),
            shape((lat, 1), F32),
        ),
        in_specs=[VMEM] * 6,
        out_specs=(VMEM,) * 4,
        compiler_params=PARAMS,
        scratch_shapes=[pltpu.VMEM((total_rows, width), F32)],
    )(near, other, w_enc, bias, w_dec, norm)
    pair = keep + swap(send, "tensor", n_tensor, 1)
    share = pair[0]
    for part in swaps(list(pair[1:]), "tensor", n_tensor, masks[1:]):
        share = share + part
    across = range(1, n_section)
    terms = [share] + swaps([share] * n_section, "section", n_section, across)
    packed = width // 2 + width // rows + LANES
    recon, payload = pl.pallas_call(
        functools.partial(error_kernel, n_tensor, len(terms)),
        out_shape=(shape((rows, width), F32), shape((2 * rows, packed), BF16)),
        in_specs=[VMEM] * (len(terms) + 2),
        out_specs=(VMEM, VMEM),
        compiler_params=PARAMS,
        scratch_shapes=[pltpu.VMEM((2 * rows, packed), F32)],
    )(*terms, b_dec.reshape(1, width), own)
    near = jnp.stack([payload] + swaps([payload] * half, "tensor", n_tensor, masks[1:]))
    other = swap(near, "tensor", n_tensor, 1)
    chunk = chunk_of(width)
    grad_w_dec, code_grad, column, loss = pl.pallas_call(
        functools.partial(backward_kernel, order),
        out_shape=(
            shape((lat, width), BF16),
            shape((total_rows, lat) if rows % 4 == 0 else (n_tensor, rows, lat), F32),
            shape((width,), F32),
            shape((1, 1), F32),
        ),
        in_specs=[VMEM] * 6,
        out_specs=(pl.BlockSpec(memory_space=pl.ANY), VMEM, VMEM, VMEM),
        compiler_params=PARAMS,
        scratch_shapes=[
            pltpu.VMEM((total_rows, width), F32),
            pltpu.VMEM((width // chunk, lat, chunk), BF16),
            pltpu.SemaphoreType.DMA((width // chunk,)),
        ],
    )(near, other, codes, scale, w_dec, norm)
    return recon, grad_w_dec, code_grad.reshape(total_rows, lat), column, loss.reshape(())


def solution(mesh):
    n_section, n_tensor = mesh.shape["section"], mesh.shape["tensor"]
    in_specs = (
        P("tensor", None),
        P(("section", "tensor"), None),
        P(("section", "tensor")),
        P(("section", "tensor"), None),
        P(),
    )
    out_specs = (
        P("tensor", None),
        P(("section", "tensor"), None),
        P(None, ("section", "tensor")),
        P(),
        P(),
    )

    def body(*args):
        return per_device(n_section, n_tensor, *args)

    return jax.shard_map(body, mesh=mesh, in_specs=in_specs, out_specs=out_specs, check_vma=False)
```

```python
import functools

import jax
import jax.numpy as jnp
from jax import lax
from jax.experimental import pallas as pl
from jax.experimental.pallas import tpu as pltpu
from jax.sharding import PartitionSpec as P


epsilon = 1e-06
LANES = 128


BF16, F32 = jnp.bfloat16, jnp.float32
VMEM = pl.BlockSpec(memory_space=pltpu.VMEM)
PARAMS = pltpu.CompilerParams(vmem_limit_bytes=16 << 20)


def swap(x, axis, size, mask):
    return lax.ppermute(x, axis, [(i, i ^ mask) for i in range(size)])


def swaps(xs, axis, size, masks):
    out = []
    for x, m in zip(xs, masks):
        out.append(swap(x, axis, size, m))
    return out


def far_masks(size):
    return [0] + list(range(3, size, 2))


def tree_sum(terms):
    while len(terms) > 1:
        terms = [terms[i] + terms[i + 1] for i in range(0, len(terms), 2)]
    return terms[0]


def chunk_of(width):
    return next(c for c in (512, 384, 256, 128) if width % c == 0)


def contract(a, b, dims):
    return lax.dot_general(a, b, (dims, ((), ())), preferred_element_type=F32)


def prepare_kernel(
    dec_hbm, enc_hbm, bias_hbm, resid_hbm,
    dec_ref, enc_ref, norm_ref, bias_col_ref, own_ref, bias_buf, sems,
):
    lat, width = dec_ref.shape
    pairs = ((bias_hbm, bias_buf), (dec_hbm, dec_ref), (resid_hbm, own_ref), (enc_hbm, enc_ref))
    copies = [pltpu.make_async_copy(a, b, sems.at[k]) for k, (a, b) in enumerate(pairs)]
    for copy in copies:
        copy.start()
    copies[0].wait()
    bias_col_ref[...] = jnp.transpose(jnp.broadcast_to(bias_buf[...], (8, lat)))[:, :1]
    copies[1].wait()
    total = jnp.zeros((lat, LANES), F32)
    for c in range(0, width, LANES):
        part = dec_ref[:, c : c + LANES].astype(F32)
        total = total + part * part
    norm_ref[...] = jnp.sqrt(jnp.sum(total, axis=1, keepdims=True) + epsilon)
    copies[2].wait()
    copies[3].wait()


def decode_half(by_row, dec_ref, tail, out_ref):
    half, rows, wide = out_ref.shape
    width = wide - LANES
    for k in range(half):
        out_ref[k, :, width:] = tail
    chunk = chunk_of(width)
    for c in range(0, width, chunk):
        part = contract(by_row, dec_ref[:, c : c + chunk], ((1,), (0,)))
        for k in range(half):
            out_ref[k, :, c : c + chunk] = part[k * rows : (k + 1) * rows]


def encode_kernel(
    near_ref, other_ref, enc_ref, bias_ref, dec_ref, norm_ref,
    send_ref, near_codes_ref, tail_ref, codes_ref, scale_ref, rows_f32,
):
    half, rows, _ = near_ref.shape
    for p in range(2 * half):
        block = near_ref[p] if p < half else other_ref[p - half]
        rows_f32[p * rows : (p + 1) * rows, :] = block.astype(F32)
    stream = rows_f32[...].astype(BF16)
    preact = contract(enc_ref[...], stream, ((1,), (1,))) + bias_ref[...]
    codes = jnp.maximum(preact, 0.0).astype(BF16)
    codes_ref[...] = codes
    codes_f32 = codes.astype(F32)
    norm = norm_ref[...]
    scale_ref[...] = jnp.sum(codes_f32, axis=1, keepdims=True) / norm
    penalty = jnp.sum(codes_f32 * norm, axis=(0, 1), keepdims=True)
    tail = jnp.broadcast_to(penalty, (rows, LANES))
    tail_ref[...] = tail
    by_row = jnp.transpose(codes_f32)
    near_codes_ref[...] = by_row[: half * rows].astype(BF16)
    decode_half(by_row[half * rows :].astype(BF16), dec_ref, tail, send_ref)


def keep_kernel(near_codes_ref, tail_ref, dec_ref, keep_ref):
    decode_half(near_codes_ref[...], dec_ref, tail_ref[...], keep_ref)


def recon_of(terms, bias_ref):
    total = tree_sum([t[...] for t in terms])
    width = bias_ref.shape[1]
    return total[:, :width] + bias_ref[...], total[:1, width:]


def recon_kernel(n_terms, *refs):
    terms, (bias_ref, recon_ref) = refs[:n_terms], refs[n_terms:]
    recon_ref[...] = recon_of(terms, bias_ref)[0]


def error_kernel(n_tensor, n_terms, *refs):
    terms, (bias_ref, resid_ref, out_ref, pack) = refs[:n_terms], refs[n_terms:]
    rows, width = resid_ref.shape
    cut, piece = width // 2, width // rows
    recon, penalty = recon_of(terms, bias_ref)
    errors = recon - resid_ref[...].astype(F32)
    column = jnp.sum(errors, axis=0, keepdims=True)
    squares = jnp.zeros((rows, LANES), F32)
    for c in range(0, width, LANES):
        squares = squares + errors[:, c : c + LANES] * errors[:, c : c + LANES]
    value = 0.5 * jnp.sum(squares, axis=0, keepdims=True) + penalty * (1.0 / (n_tensor * LANES))
    pack[:rows, :cut] = errors[:, :cut]
    pack[rows:, :cut] = errors[:, cut:]
    high = column.astype(BF16).astype(F32)
    low = column - high
    for r in range(rows):
        pack[r : r + 1, cut : cut + piece] = high[:, r * piece : (r + 1) * piece]
        pack[rows + r : rows + r + 1, cut : cut + piece] = low[:, r * piece : (r + 1) * piece]
    pack[:, cut + piece :] = jnp.zeros((2 * rows, LANES), F32)
    for r in range(3):
        high = value.astype(BF16).astype(F32)
        pack[r : r + 1, cut + piece :] = high
        value = value - high
    out_ref[...] = pack[...].astype(BF16)


def backward_kernel(
    order, near_ref, other_ref, codes_ref, scale_ref, dec_ref, norm_ref,
    grad_ref, code_grad_ref, column_ref, loss_ref,
    errors_ref, staged, by_row_ref, column_buf, loss_buf, sems, small_sems,
):
    half, rows2, _ = near_ref.shape
    rows = rows2 // 2
    _, width = dec_ref.shape
    cut, piece = width // 2, width // rows
    blocks = [near_ref.at[p] if p < half else other_ref.at[p - half] for p in range(2 * half)]
    codes, scale = codes_ref[...], scale_ref[...]
    chunk = staged.shape[2]
    copies = []

    def write(source, target, sem):
        copies.append(pltpu.make_async_copy(source, target, sem))
        copies[-1].start()

    for i in range(width // chunk):
        cols = slice(i * chunk, (i + 1) * chunk)
        low = i * chunk % cut
        first = rows * (i * chunk // cut)
        part = [b[:, low : low + chunk].astype(F32)[first : first + rows] for b in blocks]
        errors = jnp.concatenate(part).astype(BF16)
        errors_ref[:, cols] = errors
        grad = contract(codes, errors, ((1,), (0,)))
        staged[i] = (grad + scale * dec_ref[:, cols].astype(F32)).astype(BF16)
        write(staged.at[i], grad_ref.at[:, cols], sems.at[i])

    by_lat = contract(dec_ref[...], errors_ref[...], ((1,), (1,))) + norm_ref[...]
    by_row = jnp.transpose(by_lat)
    me = lax.axis_index("tensor")
    for p, mask in enumerate(order[:half]):
        block = lax.bitwise_xor(me, mask)
        one = by_row[p * rows : (p + 1) * rows]
        two = by_row[(half + p) * rows : (half + p + 1) * rows]
        if len(by_row_ref.shape) == 3:
            by_row_ref[block] = one
            by_row_ref[lax.bitwise_xor(block, 1)] = two
        else:
            odd = lax.rem(block, 2) == 1
            both = jnp.concatenate([jnp.where(odd, two, one), jnp.where(odd, one, two)])
            start = pl.multiple_of(lax.div(block, 2) * 2 * rows, 2 * rows)
            by_row_ref[pl.ds(start, 2 * rows), :] = both
    write(by_row_ref, code_grad_ref, small_sems.at[0])

    columns, losses = {}, {}
    for p, mask in enumerate(order):
        ends = blocks[p][:, cut:].astype(F32)
        columns[mask] = ends[:rows, :piece] + ends[rows:, :piece]
        losses[mask] = (ends[0:1, piece:] + ends[1:2, piece:]) + ends[2:3, piece:]
    column = tree_sum([columns[m] for m in range(len(order))])
    for r in range(rows):
        column_buf[r * piece : (r + 1) * piece] = column[r]
    write(column_buf, column_ref, small_sems.at[1])
    loss = tree_sum([losses[m] for m in range(len(order))])
    loss_buf[...] = jnp.sum(loss, axis=1, keepdims=True) / (len(order) * rows * width)
    write(loss_buf, loss_ref, small_sems.at[2])
    for copy in copies:
        copy.wait()


def per_device(n_section, n_tensor, resid, w_enc, b_enc, w_dec, b_dec):
    rows, width = resid.shape
    lat = w_enc.shape[0]
    masks = far_masks(n_tensor)
    order = masks + [m ^ 1 for m in masks]
    half = len(masks)
    total_rows = n_tensor * rows
    wide = width + LANES
    shape = jax.ShapeDtypeStruct

    anywhere = pl.BlockSpec(memory_space=pl.ANY)
    stored = [
        pltpu.with_memory_space_constraint(x, pltpu.HBM)
        for x in (w_dec, w_enc, b_enc.reshape(1, lat), resid)
    ]
    w_dec, w_enc, norm, bias, own = pl.pallas_call(
        prepare_kernel,
        out_shape=(
            shape((lat, width), BF16),
            shape((lat, width), BF16),
            shape((lat, 1), F32),
            shape((lat, 1), F32),
            shape((rows, width), BF16),
        ),
        in_specs=[anywhere] * 4,
        out_specs=(VMEM,) * 5,
        compiler_params=PARAMS,
        scratch_shapes=[pltpu.VMEM((1, lat), F32), pltpu.SemaphoreType.DMA((4,))],
    )(*stored)
    near = jnp.stack([own] + swaps([resid] * half, "tensor", n_tensor, masks[1:]))
    near, norm = lax.optimization_barrier((near, norm))
    other = swap(near, "tensor", n_tensor, 1)
    send, near_codes, tail, codes, scale = pl.pallas_call(
        encode_kernel,
        out_shape=(
            shape((half, rows, wide), F32),
            shape((half * rows, lat), BF16),
            shape((rows, LANES), F32),
            shape((lat, total_rows), BF16),
            shape((lat, 1), F32),
        ),
        in_specs=[VMEM] * 6,
        out_specs=(VMEM,) * 5,
        compiler_params=PARAMS,
        scratch_shapes=[pltpu.VMEM((total_rows, width), F32)],
    )(near, other, w_enc, bias, w_dec, norm)
    (received,) = swaps([send], "tensor", n_tensor, [1])
    keep = pl.pallas_call(
        keep_kernel,
        out_shape=shape((half, rows, wide), F32),
        in_specs=[VMEM] * 3,
        out_specs=VMEM,
        compiler_params=PARAMS,
    )(near_codes, tail, w_dec)
    pair = keep + received
    share = pair[0]
    for part in swaps(list(pair[1:]), "tensor", n_tensor, masks[1:]):
        share = share + part
    across = range(1, n_section)
    terms = [share] + swaps([share] * n_section, "section", n_section, across)
    packed = width // 2 + width // rows + LANES
    bias = b_dec.reshape(1, width)
    payload = pl.pallas_call(
        functools.partial(error_kernel, n_tensor, len(terms)),
        out_shape=shape((2 * rows, packed), BF16),
        in_specs=[VMEM] * (len(terms) + 2),
        out_specs=VMEM,
        compiler_params=PARAMS,
        scratch_shapes=[pltpu.VMEM((2 * rows, packed), F32)],
    )(*terms, bias, own)
    near = jnp.stack([payload] + swaps([payload] * half, "tensor", n_tensor, masks[1:]))
    recon = pl.pallas_call(
        functools.partial(recon_kernel, len(terms)),
        out_shape=shape((rows, width), F32),
        in_specs=[VMEM] * (len(terms) + 1),
        out_specs=VMEM,
        compiler_params=PARAMS,
    )(*terms, bias)
    other = swap(near, "tensor", n_tensor, 1)
    chunk = chunk_of(width // 2)
    n_chunks = width // chunk
    by_row = (total_rows, lat) if rows % 4 == 0 else (n_tensor, rows, lat)
    grad_w_dec, code_grad, column, loss = pl.pallas_call(
        functools.partial(backward_kernel, order),
        out_shape=(
            shape((lat, width), BF16),
            shape(by_row, F32),
            shape((width,), F32),
            shape((1, 1), F32),
        ),
        in_specs=[VMEM] * 6,
        out_specs=(anywhere,) * 4,
        compiler_params=PARAMS,
        scratch_shapes=[
            pltpu.VMEM((total_rows, width), BF16),
            pltpu.VMEM((n_chunks, lat, chunk), BF16),
            pltpu.VMEM(by_row, F32),
            pltpu.VMEM((width,), F32),
            pltpu.VMEM((1, 1), F32),
            pltpu.SemaphoreType.DMA((n_chunks,)),
            pltpu.SemaphoreType.DMA((3,)),
        ],
    )(near, other, codes, scale, w_dec, norm)
    return recon, grad_w_dec, code_grad.reshape(total_rows, lat), column, loss.reshape(())


def solution(mesh):
    n_section, n_tensor = mesh.shape["section"], mesh.shape["tensor"]
    in_specs = (
        P("tensor", None),
        P(("section", "tensor"), None),
        P(("section", "tensor")),
        P(("section", "tensor"), None),
        P(),
    )
    out_specs = (
        P("tensor", None),
        P(("section", "tensor"), None),
        P(None, ("section", "tensor")),
        P(),
        P(),
    )

    def body(*args):
        return per_device(n_section, n_tensor, *args)

    return jax.shard_map(body, mesh=mesh, in_specs=in_specs, out_specs=out_specs, check_vma=False)
```

```python
import functools

import jax
import jax.numpy as jnp
from jax import lax
from jax.experimental import pallas as pl
from jax.experimental.pallas import tpu as pltpu
from jax.sharding import PartitionSpec as P


epsilon = 1e-06
LANES = 128


BF16, F32 = jnp.bfloat16, jnp.float32
VMEM = pl.BlockSpec(memory_space=pltpu.VMEM)
PARAMS = pltpu.CompilerParams(vmem_limit_bytes=16 << 20)


def swap(x, axis, size, mask):
    return lax.ppermute(x, axis, [(i, i ^ mask) for i in range(size)])


def swaps(xs, axis, size, masks):
    out = []
    for x, m in zip(xs, masks):
        out.append(swap(x, axis, size, m))
    return out


def far_masks(size):
    return [0] + list(range(3, size, 2))


def tree_sum(terms):
    while len(terms) > 1:
        terms = [terms[i] + terms[i + 1] for i in range(0, len(terms), 2)]
    return terms[0]


def chunk_of(width):
    return next(c for c in (512, 384, 256, 128) if width % c == 0)


def contract(a, b, dims):
    return lax.dot_general(a, b, (dims, ((), ())), preferred_element_type=F32)


def fetch_kernel(dec_hbm, enc_hbm, bias_hbm, resid_hbm, dec_ref, enc_ref, bias_ref, own_ref, sems):
    pairs = ((enc_hbm, enc_ref), (dec_hbm, dec_ref), (bias_hbm, bias_ref), (resid_hbm, own_ref))
    copies = [pltpu.make_async_copy(a, b, sems.at[k]) for k, (a, b) in enumerate(pairs)]
    for copy in copies:
        copy.start()
    for copy in copies:
        copy.wait()


def forward_kernel(half, *refs):
    blocks, refs = refs[:half], refs[half:]
    encs, biases, dec_ref = refs[0:2], refs[2:4], refs[4]
    part_ref, codes_refs = refs[5], refs[6:]
    rows, width = blocks[0].shape
    lat = encs[0].shape[0]
    chunk = chunk_of(width)
    by_lat = [jnp.zeros((lat, half * rows), F32) for _ in encs]
    for c in range(0, width, chunk):
        stream = jnp.concatenate([b[:, c : c + chunk].astype(F32) for b in blocks]).astype(BF16)
        for k, enc in enumerate(encs):
            by_lat[k] = by_lat[k] + contract(enc[:, c : c + chunk], stream, ((1,), (1,)))
    for k, codes_ref in enumerate(codes_refs):
        preact = jnp.transpose(by_lat[k]) + biases[k][...]
        codes_ref[...] = jnp.maximum(preact, 0.0).astype(BF16)
    for c in range(0, width, chunk):
        cols = slice(c, c + chunk)
        part_ref[:, cols] = contract(codes_refs[0][...], dec_ref[:, cols], ((1,), (0,)))


def mate_kernel(part_ref, codes_ref, dec_ref, *shares):
    rows, width = shares[0].shape
    chunk = chunk_of(width)
    for c in range(0, width, chunk):
        cols = slice(c, c + chunk)
        total = part_ref[:, cols] + contract(codes_ref[...], dec_ref[:, cols], ((1,), (0,)))
        for k, share in enumerate(shares):
            share[:, cols] = total[k * rows : (k + 1) * rows]


def norm_of(dec_ref):
    lat, width = dec_ref.shape
    total = jnp.zeros((lat, LANES), F32)
    for c in range(0, width, LANES):
        part = dec_ref[:, c : c + LANES].astype(F32)
        total = total + part * part
    return jnp.sqrt(jnp.sum(total, axis=1, keepdims=True) + epsilon)


def norms_kernel(dec_ref, dec2_ref, codes_ref, codes2_ref, norm_ref, tail_ref):
    lat = dec_ref.shape[0]
    penalty = jnp.zeros((1, 1), F32)
    for k, (dec, codes) in enumerate(((dec_ref, codes_ref), (dec2_ref, codes2_ref))):
        norm = norm_of(dec)
        if k == 0:
            norm_ref[...] = norm
        by_lat = jnp.transpose(jnp.broadcast_to(norm, (lat, LANES)))[:1]
        each = jnp.sum(codes[...].astype(F32), axis=0, keepdims=True) * by_lat
        penalty = penalty + jnp.sum(each, axis=1, keepdims=True)
    tail_ref[...] = jnp.broadcast_to(penalty, tail_ref.shape)


def share_kernel(*refs):
    terms, (tail_ref, out_ref) = refs[:-2], refs[-2:]
    width = terms[0].shape[1]
    total = terms[0][...]
    for term in terms[1:]:
        total = total + term[...]
    out_ref[:, :width] = total
    out_ref[:, width:] = tail_ref[...]


def ready_kernel(codes_ref, others_ref, dec_ref, norm_ref, by_lat_ref, scale_ref, turned_ref, row_ref):
    lat, width = dec_ref.shape
    codes = jnp.transpose(jnp.concatenate([r[...].astype(F32) for r in (codes_ref, others_ref)]))
    by_lat_ref[...] = codes.astype(BF16)
    norm = norm_ref[...]
    scale_ref[...] = jnp.sum(codes, axis=1, keepdims=True) / norm
    row_ref[...] = jnp.transpose(jnp.broadcast_to(norm, (lat, LANES)))[:1]
    chunk = chunk_of(width)
    for c in range(0, width, chunk):
        turned_ref[c : c + chunk, :] = jnp.transpose(dec_ref[:, c : c + chunk])


def recon_of(terms, bias_ref):
    total = tree_sum([t[...] for t in terms])
    width = bias_ref.shape[1]
    return total[:, :width] + bias_ref[...], total[:1, width:]


def recon_kernel(n_terms, *refs):
    terms, (bias_ref, recon_ref) = refs[:n_terms], refs[n_terms:]
    recon_ref[...] = recon_of(terms, bias_ref)[0]


def error_kernel(n_terms, *refs):
    terms, (bias_ref, resid_ref, out_ref, pack) = refs[:n_terms], refs[n_terms:]
    rows, width = resid_ref.shape
    cut, piece = width // 2, width // rows
    recon, penalty = recon_of(terms, bias_ref)
    errors = recon - resid_ref[...].astype(F32)
    column = jnp.sum(errors, axis=0, keepdims=True)
    squares = jnp.zeros((rows, LANES), F32)
    for c in range(0, width, LANES):
        squares = squares + errors[:, c : c + LANES] * errors[:, c : c + LANES]
    value = 0.5 * jnp.sum(squares, axis=0, keepdims=True) + penalty * (1.0 / LANES)
    pack[:rows, :cut] = errors[:, :cut]
    pack[rows:, :cut] = errors[:, cut:]
    high = column.astype(BF16).astype(F32)
    low = column - high
    for r in range(rows):
        pack[r : r + 1, cut : cut + piece] = high[:, r * piece : (r + 1) * piece]
        pack[rows + r : rows + r + 1, cut : cut + piece] = low[:, r * piece : (r + 1) * piece]
    pack[:, cut + piece :] = jnp.zeros((2 * rows, LANES), F32)
    for r in range(3):
        high = value.astype(BF16).astype(F32)
        pack[r : r + 1, cut + piece :] = high
        value = value - high
    out_ref[...] = pack[...].astype(BF16)


def backward_kernel(
    order, near_ref, other_ref, codes_ref, scale_ref, dec_ref, turned_ref, norm_ref,
    grad_ref, code_grad_ref, column_ref, loss_ref,
    errors_ref, staged, by_row_ref, column_buf, loss_buf, sems, small_sems,
):
    half, rows2, _ = near_ref.shape
    rows = rows2 // 2
    lat, width = dec_ref.shape
    cut, piece = width // 2, width // rows
    blocks = [near_ref.at[p] if p < half else other_ref.at[p - half] for p in range(2 * half)]
    codes, scale = codes_ref[...], scale_ref[...]
    n_chunks, _, chunk = staged.shape
    copies = []

    def write(source, target, sem):
        copies.append(pltpu.make_async_copy(source, target, sem))
        copies[-1].start()

    def write_grad(i):
        cols = slice(i * chunk, (i + 1) * chunk)
        grad = contract(codes, errors_ref[:, cols], ((1,), (0,)))
        staged[i] = (grad + scale * dec_ref[:, cols].astype(F32)).astype(BF16)
        write(staged.at[i], grad_ref.at[:, cols], sems.at[i])

    for i in range(n_chunks):
        low = i * chunk % cut
        first = rows * (i * chunk // cut)
        part = [b[:, low : low + chunk].astype(F32)[first : first + rows] for b in blocks]
        errors_ref[:, i * chunk : (i + 1) * chunk] = jnp.concatenate(part).astype(BF16)
    for i in range(n_chunks // 2):
        write_grad(i)

    by_row = jnp.broadcast_to(norm_ref[...], (2 * half * rows, lat))
    step = chunk_of(width)
    for c in range(0, width, step):
        by_row = by_row + contract(errors_ref[:, c : c + step], turned_ref[c : c + step], ((1,), (0,)))
    me = lax.axis_index("tensor")
    for p, mask in enumerate(order[:half]):
        block = lax.bitwise_xor(me, mask)
        one = by_row[p * rows : (p + 1) * rows]
        two = by_row[(half + p) * rows : (half + p + 1) * rows]
        if len(by_row_ref.shape) == 3:
            by_row_ref[block] = one
            by_row_ref[lax.bitwise_xor(block, 1)] = two
        else:
            odd = lax.rem(block, 2) == 1
            both = jnp.concatenate([jnp.where(odd, two, one), jnp.where(odd, one, two)])
            start = pl.multiple_of(lax.div(block, 2) * 2 * rows, 2 * rows)
            by_row_ref[pl.ds(start, 2 * rows), :] = both
    write(by_row_ref, code_grad_ref, small_sems.at[0])
    for i in range(n_chunks // 2, n_chunks):
        write_grad(i)

    columns, losses = {}, {}
    for p, mask in enumerate(order):
        ends = blocks[p][:, cut:].astype(F32)
        columns[mask] = ends[:rows, :piece] + ends[rows:, :piece]
        losses[mask] = (ends[0:1, piece:] + ends[1:2, piece:]) + ends[2:3, piece:]
    column = tree_sum([columns[m] for m in range(len(order))])
    for r in range(rows):
        column_buf[r * piece : (r + 1) * piece] = column[r]
    write(column_buf, column_ref, small_sems.at[1])
    loss = tree_sum([losses[m] for m in range(len(order))])
    loss_buf[...] = jnp.sum(loss, axis=1, keepdims=True) / (len(order) * rows * width)
    write(loss_buf, loss_ref, small_sems.at[2])
    for copy in copies:
        copy.wait()


def per_device(n_section, n_tensor, resid, w_enc, b_enc, w_dec, b_dec):
    rows, width = resid.shape
    lat = w_enc.shape[0]
    masks = far_masks(n_tensor)
    order = masks + [m ^ 1 for m in masks]
    half = len(masks)
    total_rows = n_tensor * rows
    wide = width + LANES
    shape = jax.ShapeDtypeStruct

    anywhere = pl.BlockSpec(memory_space=pl.ANY)
    anywhere = pl.BlockSpec(memory_space=pl.ANY)
    bias = b_enc.reshape(1, lat)
    stored = [pltpu.with_memory_space_constraint(x, pltpu.HBM) for x in (w_dec, w_enc, bias, resid)]

    def mate(x):
        return swaps([x], "tensor", n_tensor, [1])[0]

    def call(kernel, outs, *args, **kwargs):
        return pl.pallas_call(
            kernel,
            out_shape=tuple(outs),
            in_specs=[VMEM] * len(args),
            out_specs=(VMEM,) * len(outs),
            compiler_params=PARAMS,
            **kwargs,
        )(*args)

    enc2, dec2, bias2 = mate(w_enc), mate(w_dec), mate(bias)
    w_dec, w_enc, bias, own = pl.pallas_call(
        fetch_kernel,
        out_shape=tuple(shape(x.shape, x.dtype) for x in (w_dec, w_enc, bias, resid)),
        in_specs=[anywhere] * 4,
        out_specs=(VMEM,) * 4,
        compiler_params=PARAMS,
        scratch_shapes=[pltpu.SemaphoreType.DMA((4,))],
    )(*stored)
    blocks = [own] + swaps([resid] * half, "tensor", n_tensor, masks[1:])
    part, codes, codes2 = call(
        functools.partial(forward_kernel, half),
        [shape((half * rows, width), F32)] + [shape((half * rows, lat), BF16)] * 2,
        *blocks, w_enc, enc2, bias, bias2, w_dec,
    )
    shares = call(mate_kernel, [shape((rows, width), F32)] * half, part, codes2, dec2)
    received = swaps(shares[1:], "tensor", n_tensor, masks[1:])
    norm, tail = call(
        norms_kernel,
        [shape((lat, 1), F32), shape((rows, LANES), F32)],
        w_dec, dec2, codes, codes2,
    )
    (share,) = call(share_kernel, [shape((rows, wide), F32)], shares[0], *received, tail)
    across = range(1, n_section)
    terms = [share] + swaps([share] * n_section, "section", n_section, across)
    by_lat, scale, turned, norm = call(
        ready_kernel,
        [
            shape((lat, total_rows), BF16),
            shape((lat, 1), F32),
            shape((width, lat), BF16),
            shape((1, lat), F32),
        ],
        codes, mate(codes2), w_dec, norm,
    )
    packed = width // 2 + width // rows + LANES
    bias = b_dec.reshape(1, width)
    payload = pl.pallas_call(
        functools.partial(error_kernel, len(terms)),
        out_shape=shape((2 * rows, packed), BF16),
        in_specs=[VMEM] * (len(terms) + 2),
        out_specs=VMEM,
        compiler_params=PARAMS,
        scratch_shapes=[pltpu.VMEM((2 * rows, packed), F32)],
    )(*terms, bias, own)
    near = jnp.stack([payload] + swaps([payload] * half, "tensor", n_tensor, masks[1:]))
    recon = pl.pallas_call(
        functools.partial(recon_kernel, len(terms)),
        out_shape=shape((rows, width), F32),
        in_specs=[VMEM] * (len(terms) + 1),
        out_specs=VMEM,
        compiler_params=PARAMS,
    )(*terms, bias)
    other = swap(near, "tensor", n_tensor, 1)
    chunk = width // 4
    n_chunks = width // chunk
    by_row = (total_rows, lat) if rows % 4 == 0 else (n_tensor, rows, lat)
    grad_w_dec, code_grad, column, loss = pl.pallas_call(
        functools.partial(backward_kernel, order),
        out_shape=(
            shape((lat, width), BF16),
            shape(by_row, F32),
            shape((width,), F32),
            shape((1, 1), F32),
        ),
        in_specs=[VMEM] * 7,
        out_specs=(anywhere,) * 4,
        compiler_params=PARAMS,
        scratch_shapes=[
            pltpu.VMEM((total_rows, width), BF16),
            pltpu.VMEM((n_chunks, lat, chunk), BF16),
            pltpu.VMEM(by_row, F32),
            pltpu.VMEM((width,), F32),
            pltpu.VMEM((1, 1), F32),
            pltpu.SemaphoreType.DMA((n_chunks,)),
            pltpu.SemaphoreType.DMA((3,)),
        ],
    )(near, other, by_lat, scale, w_dec, turned, norm)
    return recon, grad_w_dec, code_grad.reshape(total_rows, lat), column, loss.reshape(())


def solution(mesh):
    n_section, n_tensor = mesh.shape["section"], mesh.shape["tensor"]
    in_specs = (
        P("tensor", None),
        P(("section", "tensor"), None),
        P(("section", "tensor")),
        P(("section", "tensor"), None),
        P(),
    )
    out_specs = (
        P("tensor", None),
        P(("section", "tensor"), None),
        P(None, ("section", "tensor")),
        P(),
        P(),
    )

    def body(*args):
        return per_device(n_section, n_tensor, *args)

    return jax.shard_map(body, mesh=mesh, in_specs=in_specs, out_specs=out_specs, check_vma=False)
```

```python
import functools

import jax
import jax.numpy as jnp
from jax import lax
from jax.experimental import pallas as pl
from jax.experimental.pallas import tpu as pltpu
from jax.sharding import PartitionSpec as P


epsilon = 1e-06
LANES = 128


BF16, F32 = jnp.bfloat16, jnp.float32
VMEM = pl.BlockSpec(memory_space=pltpu.VMEM)
PARAMS = pltpu.CompilerParams(vmem_limit_bytes=16 << 20)


def swap(x, axis, size, mask):
    return lax.ppermute(x, axis, [(i, i ^ mask) for i in range(size)])


def swaps(xs, axis, size, masks):
    out = []
    for x, m in zip(xs, masks):
        out.append(swap(x, axis, size, m))
    return out


def far_masks(size):
    return [0] + list(range(3, size, 2))


def tree_sum(terms):
    while len(terms) > 1:
        terms = [terms[i] + terms[i + 1] for i in range(0, len(terms), 2)]
    return terms[0]


def chunk_of(width):
    return next(c for c in (512, 384, 256, 128) if width % c == 0)


def contract(a, b, dims):
    return lax.dot_general(a, b, (dims, ((), ())), preferred_element_type=F32)


def fetch_kernel(dec_hbm, enc_hbm, bias_hbm, resid_hbm, dec_ref, enc_ref, bias_ref, own_ref, sems):
    pairs = ((enc_hbm, enc_ref), (dec_hbm, dec_ref), (bias_hbm, bias_ref), (resid_hbm, own_ref))
    copies = [pltpu.make_async_copy(a, b, sems.at[k]) for k, (a, b) in enumerate(pairs)]
    for copy in copies:
        copy.start()
    for copy in copies:
        copy.wait()


def forward_kernel(half, *refs):
    blocks, refs = refs[:half], refs[half:]
    encs, biases, decs = refs[0:2], refs[2:4], refs[4:6]
    shares, codes_refs = refs[6 : 6 + half], refs[6 + half :]
    rows, width = blocks[0].shape
    lat = encs[0].shape[0]
    chunk = chunk_of(width)
    by_lat = [jnp.zeros((lat, half * rows), F32) for _ in encs]
    for c in range(0, width, chunk):
        stream = jnp.concatenate([b[:, c : c + chunk].astype(F32) for b in blocks]).astype(BF16)
        for k, enc in enumerate(encs):
            by_lat[k] = by_lat[k] + contract(enc[:, c : c + chunk], stream, ((1,), (1,)))
    for k, codes_ref in enumerate(codes_refs):
        preact = jnp.transpose(by_lat[k]) + biases[k][...]
        codes_ref[...] = jnp.maximum(preact, 0.0).astype(BF16)
    for c in range(0, width, chunk):
        cols = slice(c, c + chunk)
        part = contract(codes_refs[0][...], decs[0][:, cols], ((1,), (0,)))
        part = part + contract(codes_refs[1][...], decs[1][:, cols], ((1,), (0,)))
        for k, share in enumerate(shares):
            share[:, cols] = part[k * rows : (k + 1) * rows]


def norm_of(dec_ref):
    lat, width = dec_ref.shape
    total = jnp.zeros((lat, LANES), F32)
    for c in range(0, width, LANES):
        part = dec_ref[:, c : c + LANES].astype(F32)
        total = total + part * part
    return jnp.sqrt(jnp.sum(total, axis=1, keepdims=True) + epsilon)


def norms_kernel(dec_ref, dec2_ref, codes_ref, codes2_ref, norm_ref, tail_ref):
    lat = dec_ref.shape[0]
    penalty = jnp.zeros((1, 1), F32)
    for k, (dec, codes) in enumerate(((dec_ref, codes_ref), (dec2_ref, codes2_ref))):
        norm = norm_of(dec)
        if k == 0:
            norm_ref[...] = norm
        by_lat = jnp.transpose(jnp.broadcast_to(norm, (lat, LANES)))[:1]
        each = jnp.sum(codes[...].astype(F32), axis=0, keepdims=True) * by_lat
        penalty = penalty + jnp.sum(each, axis=1, keepdims=True)
    tail_ref[...] = jnp.broadcast_to(penalty, tail_ref.shape)


def share_kernel(*refs):
    terms, (tail_ref, out_ref) = refs[:-2], refs[-2:]
    width = terms[0].shape[1]
    total = terms[0][...]
    for term in terms[1:]:
        total = total + term[...]
    out_ref[:, :width] = total
    out_ref[:, width:] = tail_ref[...]


def ready_kernel(codes_ref, others_ref, dec_ref, norm_ref, by_lat_ref, scale_ref, turned_ref, row_ref):
    lat, width = dec_ref.shape
    codes = jnp.transpose(jnp.concatenate([r[...].astype(F32) for r in (codes_ref, others_ref)]))
    by_lat_ref[...] = codes.astype(BF16)
    norm = norm_ref[...]
    scale_ref[...] = jnp.sum(codes, axis=1, keepdims=True) / norm
    row_ref[...] = jnp.transpose(jnp.broadcast_to(norm, (lat, LANES)))[:1]
    chunk = chunk_of(width)
    for c in range(0, width, chunk):
        turned_ref[c : c + chunk, :] = jnp.transpose(dec_ref[:, c : c + chunk])


def recon_of(terms, bias_ref):
    total = tree_sum([t[...] for t in terms])
    width = bias_ref.shape[1]
    return total[:, :width] + bias_ref[...], total[:1, width:]


def recon_kernel(n_terms, *refs):
    terms, (bias_ref, recon_ref) = refs[:n_terms], refs[n_terms:]
    recon_ref[...] = recon_of(terms, bias_ref)[0]


def error_kernel(n_terms, *refs):
    terms, (bias_ref, resid_ref, out_ref, pack) = refs[:n_terms], refs[n_terms:]
    rows, width = resid_ref.shape
    cut, piece = width // 2, width // rows
    recon, penalty = recon_of(terms, bias_ref)
    errors = recon - resid_ref[...].astype(F32)
    column = jnp.sum(errors, axis=0, keepdims=True)
    squares = jnp.zeros((rows, LANES), F32)
    for c in range(0, width, LANES):
        squares = squares + errors[:, c : c + LANES] * errors[:, c : c + LANES]
    value = 0.5 * jnp.sum(squares, axis=0, keepdims=True) + penalty * (1.0 / LANES)
    pack[:rows, :cut] = errors[:, :cut]
    pack[rows:, :cut] = errors[:, cut:]
    high = column.astype(BF16).astype(F32)
    low = column - high
    for r in range(rows):
        pack[r : r + 1, cut : cut + piece] = high[:, r * piece : (r + 1) * piece]
        pack[rows + r : rows + r + 1, cut : cut + piece] = low[:, r * piece : (r + 1) * piece]
    pack[:, cut + piece :] = jnp.zeros((2 * rows, LANES), F32)
    for r in range(3):
        high = value.astype(BF16).astype(F32)
        pack[r : r + 1, cut + piece :] = high
        value = value - high
    out_ref[...] = pack[...].astype(BF16)


def backward_kernel(
    order, near_ref, other_ref, codes_ref, scale_ref, dec_ref, turned_ref, norm_ref,
    grad_ref, code_grad_ref, column_ref, loss_ref,
    errors_ref, staged, by_row_ref, column_buf, loss_buf, sems, small_sems,
):
    half, rows2, _ = near_ref.shape
    rows = rows2 // 2
    lat, width = dec_ref.shape
    cut, piece = width // 2, width // rows
    blocks = [near_ref.at[p] if p < half else other_ref.at[p - half] for p in range(2 * half)]
    codes, scale = codes_ref[...], scale_ref[...]
    n_chunks, _, chunk = staged.shape
    copies = []

    def write(source, target, sem):
        copies.append(pltpu.make_async_copy(source, target, sem))
        copies[-1].start()

    def write_grad(i):
        cols = slice(i * chunk, (i + 1) * chunk)
        grad = contract(codes, errors_ref[:, cols], ((1,), (0,)))
        staged[i] = (grad + scale * dec_ref[:, cols].astype(F32)).astype(BF16)
        write(staged.at[i], grad_ref.at[:, cols], sems.at[i])

    for i in range(n_chunks):
        low = i * chunk % cut
        first = rows * (i * chunk // cut)
        part = [b[:, low : low + chunk].astype(F32)[first : first + rows] for b in blocks]
        errors_ref[:, i * chunk : (i + 1) * chunk] = jnp.concatenate(part).astype(BF16)
    for i in range(n_chunks // 2):
        write_grad(i)

    by_row = jnp.broadcast_to(norm_ref[...], (2 * half * rows, lat))
    step = chunk_of(width)
    for c in range(0, width, step):
        by_row = by_row + contract(errors_ref[:, c : c + step], turned_ref[c : c + step], ((1,), (0,)))
    me = lax.axis_index("tensor")
    for p, mask in enumerate(order[:half]):
        block = lax.bitwise_xor(me, mask)
        one = by_row[p * rows : (p + 1) * rows]
        two = by_row[(half + p) * rows : (half + p + 1) * rows]
        if len(by_row_ref.shape) == 3:
            by_row_ref[block] = one
            by_row_ref[lax.bitwise_xor(block, 1)] = two
        else:
            odd = lax.rem(block, 2) == 1
            both = jnp.concatenate([jnp.where(odd, two, one), jnp.where(odd, one, two)])
            start = pl.multiple_of(lax.div(block, 2) * 2 * rows, 2 * rows)
            by_row_ref[pl.ds(start, 2 * rows), :] = both
    write(by_row_ref, code_grad_ref, small_sems.at[0])
    for i in range(n_chunks // 2, n_chunks):
        write_grad(i)

    columns, losses = {}, {}
    for p, mask in enumerate(order):
        ends = blocks[p][:, cut:].astype(F32)
        columns[mask] = ends[:rows, :piece] + ends[rows:, :piece]
        losses[mask] = (ends[0:1, piece:] + ends[1:2, piece:]) + ends[2:3, piece:]
    column = tree_sum([columns[m] for m in range(len(order))])
    for r in range(rows):
        column_buf[r * piece : (r + 1) * piece] = column[r]
    write(column_buf, column_ref, small_sems.at[1])
    loss = tree_sum([losses[m] for m in range(len(order))])
    loss_buf[...] = jnp.sum(loss, axis=1, keepdims=True) / (len(order) * rows * width)
    write(loss_buf, loss_ref, small_sems.at[2])
    for copy in copies:
        copy.wait()


def per_device(n_section, n_tensor, resid, w_enc, b_enc, w_dec, b_dec):
    rows, width = resid.shape
    lat = w_enc.shape[0]
    masks = far_masks(n_tensor)
    order = masks + [m ^ 1 for m in masks]
    half = len(masks)
    total_rows = n_tensor * rows
    wide = width + LANES
    shape = jax.ShapeDtypeStruct

    anywhere = pl.BlockSpec(memory_space=pl.ANY)
    anywhere = pl.BlockSpec(memory_space=pl.ANY)
    bias = b_enc.reshape(1, lat)
    stored = [pltpu.with_memory_space_constraint(x, pltpu.HBM) for x in (w_dec, w_enc, bias, resid)]

    def mate(x):
        return swaps([x], "tensor", n_tensor, [1])[0]

    def call(kernel, outs, *args, **kwargs):
        return pl.pallas_call(
            kernel,
            out_shape=tuple(outs),
            in_specs=[VMEM] * len(args),
            out_specs=(VMEM,) * len(outs),
            compiler_params=PARAMS,
            **kwargs,
        )(*args)

    enc2, dec2, bias2 = mate(w_enc), mate(w_dec), mate(bias)
    w_dec, w_enc, bias, own = pl.pallas_call(
        fetch_kernel,
        out_shape=tuple(shape(x.shape, x.dtype) for x in (w_dec, w_enc, bias, resid)),
        in_specs=[anywhere] * 4,
        out_specs=(VMEM,) * 4,
        compiler_params=PARAMS,
        scratch_shapes=[pltpu.SemaphoreType.DMA((4,))],
    )(*stored)
    blocks = [own] + swaps([resid] * half, "tensor", n_tensor, masks[1:])
    *shares, codes, codes2 = call(
        functools.partial(forward_kernel, half),
        [shape((rows, width), F32)] * half + [shape((half * rows, lat), BF16)] * 2,
        *blocks, w_enc, enc2, bias, bias2, w_dec, dec2,
    )
    received = swaps(shares[1:], "tensor", n_tensor, masks[1:])
    norm, tail = call(
        norms_kernel,
        [shape((lat, 1), F32), shape((rows, LANES), F32)],
        w_dec, dec2, codes, codes2,
    )
    (share,) = call(share_kernel, [shape((rows, wide), F32)], shares[0], *received, tail)
    across = range(1, n_section)
    terms = [share] + swaps([share] * n_section, "section", n_section, across)
    by_lat, scale, turned, norm = call(
        ready_kernel,
        [
            shape((lat, total_rows), BF16),
            shape((lat, 1), F32),
            shape((width, lat), BF16),
            shape((1, lat), F32),
        ],
        codes, mate(codes2), w_dec, norm,
    )
    packed = width // 2 + width // rows + LANES
    bias = b_dec.reshape(1, width)
    payload = pl.pallas_call(
        functools.partial(error_kernel, len(terms)),
        out_shape=shape((2 * rows, packed), BF16),
        in_specs=[VMEM] * (len(terms) + 2),
        out_specs=VMEM,
        compiler_params=PARAMS,
        scratch_shapes=[pltpu.VMEM((2 * rows, packed), F32)],
    )(*terms, bias, own)
    near = jnp.stack([payload] + swaps([payload] * half, "tensor", n_tensor, masks[1:]))
    recon = pl.pallas_call(
        functools.partial(recon_kernel, len(terms)),
        out_shape=shape((rows, width), F32),
        in_specs=[VMEM] * (len(terms) + 1),
        out_specs=VMEM,
        compiler_params=PARAMS,
    )(*terms, bias)
    other = swap(near, "tensor", n_tensor, 1)
    chunk = width // 4
    n_chunks = width // chunk
    by_row = (total_rows, lat) if rows % 4 == 0 else (n_tensor, rows, lat)
    grad_w_dec, code_grad, column, loss = pl.pallas_call(
        functools.partial(backward_kernel, order),
        out_shape=(
            shape((lat, width), BF16),
            shape(by_row, F32),
            shape((width,), F32),
            shape((1, 1), F32),
        ),
        in_specs=[VMEM] * 7,
        out_specs=(anywhere,) * 4,
        compiler_params=PARAMS,
        scratch_shapes=[
            pltpu.VMEM((total_rows, width), BF16),
            pltpu.VMEM((n_chunks, lat, chunk), BF16),
            pltpu.VMEM(by_row, F32),
            pltpu.VMEM((width,), F32),
            pltpu.VMEM((1, 1), F32),
            pltpu.SemaphoreType.DMA((n_chunks,)),
            pltpu.SemaphoreType.DMA((3,)),
        ],
    )(near, other, by_lat, scale, w_dec, turned, norm)
    return recon, grad_w_dec, code_grad.reshape(total_rows, lat), column, loss.reshape(())


def solution(mesh):
    n_section, n_tensor = mesh.shape["section"], mesh.shape["tensor"]
    in_specs = (
        P("tensor", None),
        P(("section", "tensor"), None),
        P(("section", "tensor")),
        P(("section", "tensor"), None),
        P(),
    )
    out_specs = (
        P("tensor", None),
        P(("section", "tensor"), None),
        P(None, ("section", "tensor")),
        P(),
        P(),
    )

    def body(*args):
        return per_device(n_section, n_tensor, *args)

    return jax.shard_map(body, mesh=mesh, in_specs=in_specs, out_specs=out_specs, check_vma=False)
```

```python
import functools

import jax
import jax.numpy as jnp
from jax import lax
from jax.experimental import pallas as pl
from jax.experimental.pallas import tpu as pltpu
from jax.sharding import PartitionSpec as P


epsilon = 1e-06
LANES = 128


BF16, F32 = jnp.bfloat16, jnp.float32
VMEM = pl.BlockSpec(memory_space=pltpu.VMEM)
PARAMS = pltpu.CompilerParams(vmem_limit_bytes=16 << 20)


def swap(x, axis, size, mask):
    return lax.ppermute(x, axis, [(i, i ^ mask) for i in range(size)])


def swaps(xs, axis, size, masks):
    out = []
    for x, m in zip(xs, masks):
        out.append(swap(x, axis, size, m))
    return out


def far_masks(size):
    return [0] + list(range(3, size, 2))


def tree_sum(terms):
    while len(terms) > 1:
        terms = [terms[i] + terms[i + 1] for i in range(0, len(terms), 2)]
    return terms[0]


def chunk_of(width):
    return next(c for c in (512, 384, 256, 128) if width % c == 0)


def contract(a, b, dims):
    return lax.dot_general(a, b, (dims, ((), ())), preferred_element_type=F32)


def fetch_kernel(dec_hbm, enc_hbm, bias_hbm, resid_hbm, dec_ref, enc_ref, bias_ref, own_ref, sems):
    pairs = ((enc_hbm, enc_ref), (dec_hbm, dec_ref), (bias_hbm, bias_ref), (resid_hbm, own_ref))
    copies = [pltpu.make_async_copy(a, b, sems.at[k]) for k, (a, b) in enumerate(pairs)]
    for copy in copies:
        copy.start()
    for copy in copies:
        copy.wait()


def forward_kernel(half, *refs):
    blocks, refs = refs[:half], refs[half:]
    encs, biases, decs = refs[0:2], refs[2:4], refs[4:6]
    shares, codes_refs = refs[6 : 6 + half], refs[6 + half :]
    rows, width = blocks[0].shape
    lat = encs[0].shape[0]
    chunk = chunk_of(width)
    by_lat = [jnp.zeros((lat, half * rows), F32) for _ in encs]
    for c in range(0, width, chunk):
        stream = jnp.concatenate([b[:, c : c + chunk].astype(F32) for b in blocks]).astype(BF16)
        for k, enc in enumerate(encs):
            by_lat[k] = by_lat[k] + contract(enc[:, c : c + chunk], stream, ((1,), (1,)))
    for k, codes_ref in enumerate(codes_refs):
        preact = jnp.transpose(by_lat[k]) + biases[k][...]
        codes_ref[...] = jnp.maximum(preact, 0.0).astype(BF16)
    for c in range(0, width, chunk):
        cols = slice(c, c + chunk)
        part = contract(codes_refs[0][...], decs[0][:, cols], ((1,), (0,)))
        part = part + contract(codes_refs[1][...], decs[1][:, cols], ((1,), (0,)))
        for k, share in enumerate(shares):
            share[:, cols] = part[k * rows : (k + 1) * rows]


def norm_of(dec_ref):
    lat, width = dec_ref.shape
    total = jnp.zeros((lat, LANES), F32)
    for c in range(0, width, LANES):
        part = dec_ref[:, c : c + LANES].astype(F32)
        total = total + part * part
    return jnp.sqrt(jnp.sum(total, axis=1, keepdims=True) + epsilon)


def norms_kernel(dec_ref, dec2_ref, codes_ref, codes2_ref, norm_ref, tail_ref):
    lat = dec_ref.shape[0]
    penalty = jnp.zeros((1, 1), F32)
    for k, (dec, codes) in enumerate(((dec_ref, codes_ref), (dec2_ref, codes2_ref))):
        norm = norm_of(dec)
        if k == 0:
            norm_ref[...] = norm
        by_lat = jnp.transpose(jnp.broadcast_to(norm, (lat, LANES)))[:1]
        each = jnp.sum(codes[...].astype(F32), axis=0, keepdims=True) * by_lat
        penalty = penalty + jnp.sum(each, axis=1, keepdims=True)
    tail_ref[...] = jnp.broadcast_to(penalty, tail_ref.shape)


def share_kernel(*refs):
    terms, (tail_ref, out_ref) = refs[:-2], refs[-2:]
    width = terms[0].shape[1]
    total = terms[0][...]
    for term in terms[1:]:
        total = total + term[...]
    out_ref[:, :width] = total
    out_ref[:, width:] = tail_ref[...]


def ready_kernel(codes_ref, others_ref, dec_ref, norm_ref, by_lat_ref, scale_ref, turned_ref, row_ref):
    lat, width = dec_ref.shape
    codes = jnp.transpose(jnp.concatenate([r[...].astype(F32) for r in (codes_ref, others_ref)]))
    by_lat_ref[...] = codes.astype(BF16)
    norm = norm_ref[...]
    scale_ref[...] = jnp.sum(codes, axis=1, keepdims=True) / norm
    row_ref[...] = jnp.transpose(jnp.broadcast_to(norm, (lat, LANES)))[:1]
    chunk = chunk_of(width)
    for c in range(0, width, chunk):
        turned_ref[c : c + chunk, :] = jnp.transpose(dec_ref[:, c : c + chunk])


def recon_of(terms, bias_ref):
    total = tree_sum([t[...] for t in terms])
    width = bias_ref.shape[1]
    return total[:, :width] + bias_ref[...], total[:1, width:]


def recon_kernel(n_terms, *refs):
    terms, (bias_ref, recon_ref) = refs[:n_terms], refs[n_terms:]
    recon_ref[...] = recon_of(terms, bias_ref)[0]


def error_kernel(n_terms, *refs):
    terms, (bias_ref, resid_ref, out_ref, pack) = refs[:n_terms], refs[n_terms:]
    rows, width = resid_ref.shape
    cut, piece = width // 2, width // rows
    recon, penalty = recon_of(terms, bias_ref)
    errors = recon - resid_ref[...].astype(F32)
    column = jnp.sum(errors, axis=0, keepdims=True)
    squares = jnp.zeros((rows, LANES), F32)
    for c in range(0, width, LANES):
        squares = squares + errors[:, c : c + LANES] * errors[:, c : c + LANES]
    value = 0.5 * jnp.sum(squares, axis=0, keepdims=True) + penalty * (1.0 / LANES)
    pack[:rows, :cut] = errors[:, :cut]
    pack[rows:, :cut] = errors[:, cut:]
    high = column.astype(BF16).astype(F32)
    low = column - high
    for r in range(rows):
        pack[r : r + 1, cut : cut + piece] = high[:, r * piece : (r + 1) * piece]
        pack[rows + r : rows + r + 1, cut : cut + piece] = low[:, r * piece : (r + 1) * piece]
    pack[:, cut + piece :] = jnp.zeros((2 * rows, LANES), F32)
    for r in range(3):
        high = value.astype(BF16).astype(F32)
        pack[r : r + 1, cut + piece :] = high
        value = value - high
    out_ref[...] = pack[...].astype(BF16)


def backward_kernel(order, *refs):
    blocks, refs = refs[: len(order)], refs[len(order) :]
    codes_ref, scale_ref, dec_ref, turned_ref, norm_ref = refs[:5]
    grad_ref, code_grad_ref, column_ref, loss_ref = refs[5:9]
    errors_ref, staged, by_row_ref, column_buf, loss_buf, sems, small_sems = refs[9:]
    half, rows = len(order) // 2, blocks[0].shape[0] // 2
    lat, width = dec_ref.shape
    cut, piece = width // 2, width // rows
    codes, scale = codes_ref[...], scale_ref[...]
    n_chunks, _, chunk = staged.shape
    copies = []

    def write(source, target, sem):
        copies.append(pltpu.make_async_copy(source, target, sem))
        copies[-1].start()

    def write_grad(i):
        cols = slice(i * chunk, (i + 1) * chunk)
        grad = contract(codes, errors_ref[:, cols], ((1,), (0,)))
        staged[i] = (grad + scale * dec_ref[:, cols].astype(F32)).astype(BF16)
        write(staged.at[i], grad_ref.at[:, cols], sems.at[i])

    for i in range(n_chunks):
        low = i * chunk % cut
        first = rows * (i * chunk // cut)
        part = [b[:, low : low + chunk].astype(F32)[first : first + rows] for b in blocks]
        errors_ref[:, i * chunk : (i + 1) * chunk] = jnp.concatenate(part).astype(BF16)
    for i in range(n_chunks // 2):
        write_grad(i)

    by_row = jnp.broadcast_to(norm_ref[...], (2 * half * rows, lat))
    step = width // 2
    for c in range(0, width, step):
        by_row = by_row + contract(errors_ref[:, c : c + step], turned_ref[c : c + step], ((1,), (0,)))
    me = lax.axis_index("tensor")
    for p, mask in enumerate(order[:half]):
        block = lax.bitwise_xor(me, mask)
        one = by_row[p * rows : (p + 1) * rows]
        two = by_row[(half + p) * rows : (half + p + 1) * rows]
        if len(by_row_ref.shape) == 3:
            by_row_ref[block] = one
            by_row_ref[lax.bitwise_xor(block, 1)] = two
        else:
            odd = lax.rem(block, 2) == 1
            both = jnp.concatenate([jnp.where(odd, two, one), jnp.where(odd, one, two)])
            start = pl.multiple_of(lax.div(block, 2) * 2 * rows, 2 * rows)
            by_row_ref[pl.ds(start, 2 * rows), :] = both
    write(by_row_ref, code_grad_ref, small_sems.at[0])
    for i in range(n_chunks // 2, n_chunks):
        write_grad(i)

    columns, losses = {}, {}
    for p, mask in enumerate(order):
        ends = blocks[p][:, cut:].astype(F32)
        columns[mask] = ends[:rows, :piece] + ends[rows:, :piece]
        losses[mask] = (ends[0:1, piece:] + ends[1:2, piece:]) + ends[2:3, piece:]
    column = tree_sum([columns[m] for m in range(len(order))])
    for r in range(rows):
        column_buf[r * piece : (r + 1) * piece] = column[r]
    write(column_buf, column_ref, small_sems.at[1])
    loss = tree_sum([losses[m] for m in range(len(order))])
    loss_buf[...] = jnp.sum(loss, axis=1, keepdims=True) / (len(order) * rows * width)
    write(loss_buf, loss_ref, small_sems.at[2])
    for copy in copies:
        copy.wait()


def per_device(n_section, n_tensor, resid, w_enc, b_enc, w_dec, b_dec):
    rows, width = resid.shape
    lat = w_enc.shape[0]
    masks = far_masks(n_tensor)
    order = masks + [m ^ 1 for m in masks]
    half = len(masks)
    total_rows = n_tensor * rows
    wide = width + LANES
    shape = jax.ShapeDtypeStruct

    anywhere = pl.BlockSpec(memory_space=pl.ANY)
    anywhere = pl.BlockSpec(memory_space=pl.ANY)
    bias = b_enc.reshape(1, lat)
    stored = [pltpu.with_memory_space_constraint(x, pltpu.HBM) for x in (w_dec, w_enc, bias, resid)]

    def mate(x):
        return swaps([x], "tensor", n_tensor, [1])[0]

    def call(kernel, outs, *args, **kwargs):
        return pl.pallas_call(
            kernel,
            out_shape=tuple(outs),
            in_specs=[VMEM] * len(args),
            out_specs=(VMEM,) * len(outs),
            compiler_params=PARAMS,
            **kwargs,
        )(*args)

    enc2, dec2, bias2 = mate(w_enc), mate(w_dec), mate(bias)
    w_dec, w_enc, bias, own = pl.pallas_call(
        fetch_kernel,
        out_shape=tuple(shape(x.shape, x.dtype) for x in (w_dec, w_enc, bias, resid)),
        in_specs=[anywhere] * 4,
        out_specs=(VMEM,) * 4,
        compiler_params=PARAMS,
        scratch_shapes=[pltpu.SemaphoreType.DMA((4,))],
    )(*stored)
    blocks = [own] + swaps([resid] * half, "tensor", n_tensor, masks[1:])
    *shares, codes, codes2 = call(
        functools.partial(forward_kernel, half),
        [shape((rows, width), F32)] * half + [shape((half * rows, lat), BF16)] * 2,
        *blocks, w_enc, enc2, bias, bias2, w_dec, dec2,
    )
    received = swaps(shares[1:], "tensor", n_tensor, masks[1:])
    norm, tail = call(
        norms_kernel,
        [shape((lat, 1), F32), shape((rows, LANES), F32)],
        w_dec, dec2, codes, codes2,
    )
    (share,) = call(share_kernel, [shape((rows, wide), F32)], shares[0], *received, tail)
    across = range(1, n_section)
    terms = [share] + swaps([share] * n_section, "section", n_section, across)
    by_lat, scale, turned, norm = call(
        ready_kernel,
        [
            shape((lat, total_rows), BF16),
            shape((lat, 1), F32),
            shape((width, lat), BF16),
            shape((1, lat), F32),
        ],
        codes, mate(codes2), w_dec, norm,
    )
    packed = width // 2 + width // rows + LANES
    bias = b_dec.reshape(1, width)
    payload = pl.pallas_call(
        functools.partial(error_kernel, len(terms)),
        out_shape=shape((2 * rows, packed), BF16),
        in_specs=[VMEM] * (len(terms) + 2),
        out_specs=VMEM,
        compiler_params=PARAMS,
        scratch_shapes=[pltpu.VMEM((2 * rows, packed), F32)],
    )(*terms, bias, own)
    near = [payload] + swaps([payload] * half, "tensor", n_tensor, masks[1:])
    recon = pl.pallas_call(
        functools.partial(recon_kernel, len(terms)),
        out_shape=shape((rows, width), F32),
        in_specs=[VMEM] * (len(terms) + 1),
        out_specs=VMEM,
        compiler_params=PARAMS,
    )(*terms, bias)
    other = [mate(x) for x in near]
    chunk = width // 4
    n_chunks = width // chunk
    by_row = (total_rows, lat) if rows % 4 == 0 else (n_tensor, rows, lat)
    grad_w_dec, code_grad, column, loss = pl.pallas_call(
        functools.partial(backward_kernel, order),
        out_shape=(
            shape((lat, width), BF16),
            shape(by_row, F32),
            shape((width,), F32),
            shape((1, 1), F32),
        ),
        in_specs=[VMEM] * (2 * half + 5),
        out_specs=(anywhere,) * 4,
        compiler_params=PARAMS,
        scratch_shapes=[
            pltpu.VMEM((total_rows, width), BF16),
            pltpu.VMEM((n_chunks, lat, chunk), BF16),
            pltpu.VMEM(by_row, F32),
            pltpu.VMEM((width,), F32),
            pltpu.VMEM((1, 1), F32),
            pltpu.SemaphoreType.DMA((n_chunks,)),
            pltpu.SemaphoreType.DMA((3,)),
        ],
    )(*near, *other, by_lat, scale, w_dec, turned, norm)
    return recon, grad_w_dec, code_grad.reshape(total_rows, lat), column, loss.reshape(())


def solution(mesh):
    n_section, n_tensor = mesh.shape["section"], mesh.shape["tensor"]
    in_specs = (
        P("tensor", None),
        P(("section", "tensor"), None),
        P(("section", "tensor")),
        P(("section", "tensor"), None),
        P(),
    )
    out_specs = (
        P("tensor", None),
        P(("section", "tensor"), None),
        P(None, ("section", "tensor")),
        P(),
        P(),
    )

    def body(*args):
        return per_device(n_section, n_tensor, *args)

    return jax.shard_map(body, mesh=mesh, in_specs=in_specs, out_specs=out_specs, check_vma=False)
```
